256 devices in a mesh: seq: 64 (over z_lo, y, x, core), chan: 4 (over z_hi).
Axes of the slice: x: 4, y: 4, z: 8 (z_hi: 4, z_lo: 2; z = z_hi * 2 + z_lo), core: 2. Of those that a mesh axis runs over, the one named last changes fastest.
Arguments:
- features: bfloat16 [3, 2, 8192, 8192], P(None, None, 'chan', 'seq'), may hold values from -6 to 6
- offsets: int32 [2], replicated, may hold values from 0 to 4095
- tokens: int32 [2, 4], replicated, may hold values from 0 to 511
- decay_rate: float32 [16, 8192], P(None, 'chan'), may hold values from 0 to 1
- residue: float32 [16, 8192], P(None, 'chan'), may hold values from -1 to 1
- skip_weight: float32 [8192], P('chan'), may hold values from -3 to 3
- embedding: bfloat16 [512, 8192], P(None, 'seq'), may hold values from -12 to 12
- norm_gain: float32 [8192], P('seq'), may hold values from 0.1 to 1.9
- dec_weight: bfloat16 [3, 8192, 8192], P(None, 'seq', 'chan'), may hold values from -0.1875 to 0.1875
- out_weight: bfloat16 [8192, 8192], P('chan', 'seq'), may hold values from -0.1875 to 0.1875
Outputs:
- mixed: bfloat16 [2, 8192, 8192], P(None, 'chan', 'seq')
- decoded: bfloat16 [2, 4, 8192], P(None, None, ('seq', 'chan'))
The draws below stay inside these ranges and needn't reach their ends.
All inputs are finite; a program needn't handle non-finite values.
Results may differ from the reference program's by a relative error of at most 0.0082.
Values may be sent and summed in bfloat16 or wider, within the bound.
No kernel may reach another device: no remote copies, remote signals or barrier semaphores. Data moves between devices by JAX's collectives and lax.ppermute only.
A program may use at most 128 MiB of HBM per device.

```python
import math
import jax
import jax.numpy as jnp
import numpy as np
from jax import lax

D = 8192
MODES = 16
VOCAB = 512
BATCH = 2
STEPS = 4
WINDOW = 8192


def rate_and_residue(key):
    base = jax.random.fold_in(key, 7)
    pick_key, slow_key, fast_key, res_key = jax.random.split(base, 4)
    slow_share = 0.5
    picked = jax.random.uniform(pick_key, (MODES, D), jnp.float32) < slow_share
    slow_rate = jnp.exp(jax.random.uniform(slow_key, (MODES, D), jnp.float32, math.log(0.2 / WINDOW), math.log(2.0 / WINDOW)))
    fast_rate = jnp.exp(jax.random.uniform(fast_key, (MODES, D), jnp.float32, math.log(2.0 / WINDOW), math.log(1.0 / 30.0)))
    rates = jnp.where(picked, slow_rate, fast_rate)
    noise = jnp.clip(jax.random.normal(res_key, (MODES, D), jnp.float32), -4.0, 4.0)
    residues = noise * jnp.sqrt(2.0 * rates / MODES)
    return (rates, residues)


def draw_decay_rate(key, part):
    return rate_and_residue(key)[0]


def draw_residue(key, part):
    return rate_and_residue(key)[1]


def draw_embedding(key, part):
    base = jax.random.fold_in(key, 19)
    column = jnp.arange(D, dtype=jnp.float32) / D
    values = jnp.clip(jax.random.normal(base, (VOCAB, D), jnp.float32), -4.0, 4.0) * (1.0 + 2.0 * column)
    return values.astype(jnp.bfloat16)


def touch_ends(values, key, low, top_value):
    shape = values.shape
    index_at = [jax.random.randint(jax.random.fold_in(key, axis), (), 0, shape[axis]) for axis in range(len(shape))]
    values = values.at[tuple(index_at)].set(low)
    longest = shape.index(max(shape))
    index_at[longest] = (index_at[longest] + 1) % shape[longest]
    return values.at[tuple(index_at)].set(top_value)


def strengthened(result, stream_key, source, target, parts, factor):
    def block_of(dim):
        return (jnp.arange(result.shape[dim]) // (result.shape[dim] // parts)).reshape((-1,) + (1,) * (result.ndim - 1 - dim))

    first = jax.random.permutation(stream_key, parts)[block_of(target)]
    far = (block_of(target) + parts // 2) % parts
    return jnp.where((block_of(source) == first) | (block_of(source) == far), factor * result, result)


def steps_of(stream_key, shape, cuts, smallest, high):
    factor_of, own = 1.0, jax.random.fold_in(stream_key, 6)
    for axis_at, blocks in cuts:
        draws = jnp.exp(jax.random.uniform(jax.random.fold_in(own, axis_at), (blocks,), jnp.float32, smallest / len(cuts), high / len(cuts)))
        factor_of = factor_of * jnp.repeat(draws, shape[axis_at] // blocks).reshape([-1 if axis == axis_at else 1 for axis in range(len(shape))])
    return factor_of


def rank_bounds(number_of, skew):
    portions = [(1 << 20) // math.isqrt(rank ** skew) + 1 for rank in range(1, number_of + 1)]
    spread = 1 + sum(portions) // (1 << 30)
    return np.cumsum(np.array([max(1, weight // spread) for weight in portions]))


def ranked(own_key, extent, number_of, skew):
    grid = rank_bounds(number_of, skew)
    lot = jax.random.randint(jax.random.fold_in(own_key, 1), extent, 0, int(grid[number_of - 1]))
    standing = jnp.searchsorted(jnp.asarray(grid, jnp.int32), lot, side="right")
    return jax.random.permutation(jax.random.fold_in(own_key, 2), number_of)[standing].astype(jnp.int32)


def gaussian(stream_key, shape, spread, limit, pieces=(), kind=jnp.bfloat16):
    entries = spread * jax.random.normal(stream_key, shape, jnp.float32)
    if pieces:
        entries = entries * steps_of(stream_key, shape, pieces, -0.22, 0.18)
    return jnp.clip(entries, -limit, limit).astype(kind)


def heavy_noise(own_key, dims, spread, limit, pieces, heavy, held_as=jnp.bfloat16):
    drawn = spread * jax.random.normal(own_key, dims, jnp.float32)
    if pieces:
        drawn = drawn * steps_of(own_key, dims, pieces, -0.22, 0.18)
    return jnp.clip(strengthened(drawn, jax.random.fold_in(own_key, 3), *heavy), -limit, limit).astype(held_as)


def setup_inputs(seed: int = 0) -> dict:
    splits = jax.random.split(jax.random.key(seed), 11)
    features = gaussian(splits[0], (3, BATCH, D, WINDOW), 1.0, 6.0, ((2, 4), (3, 64)))
    offsets = jax.random.randint(splits[1], (BATCH,), 0, WINDOW // 2).astype(jnp.int32)
    tokens = touch_ends(ranked(splits[2], (BATCH, STEPS), VOCAB, 2), jax.random.fold_in(splits[2], 3), 0, VOCAB - 1).astype(jnp.int32)
    decay_rate = draw_decay_rate(jax.random.fold_in(splits[10], 71), 0)
    residue = draw_residue(jax.random.fold_in(splits[10], 71), 0)
    skip_weight = gaussian(splits[5], (D,), 0.5, 3.0, ((0, 4),), jnp.float32)
    embedding = draw_embedding(jax.random.fold_in(splits[10], 71), 0)
    norm_gain = jnp.clip(1.0 + 0.18 * jax.random.normal(splits[7], (D,), jnp.float32), 0.1, 1.9)
    dec_weight = heavy_noise(splits[8], (3, D, D), D ** -0.5, 0.1875, ((1, 64), (2, 4)), (1, 2, 64, 4.0))
    out_weight = heavy_noise(splits[9], (D, D), D ** -0.5, 0.1875, ((0, 4), (1, 64)), (0, 1, 64, 4.0))
    return {"features": features, "offsets": offsets, "tokens": tokens, "decay_rate": decay_rate, "residue": residue, "skip_weight": skip_weight, "embedding": embedding, "norm_gain": norm_gain, "dec_weight": dec_weight, "out_weight": out_weight}


def reference(features, offsets, tokens, decay_rate, residue, skip_weight, embedding, norm_gain, dec_weight, out_weight):
    highest = lax.Precision.HIGHEST
    query = features[0]
    keys_in = features[1]
    values_in = features[2]
    positions = jnp.arange(WINDOW, dtype=jnp.int32)
    live = positions[None, :] >= offsets[:, None].astype(jnp.int32)
    product = jnp.where(live[:, None, :], keys_in.astype(jnp.float32) * values_in.astype(jnp.float32), jnp.float32(0.0)).astype(jnp.bfloat16)
    width = 128
    nblocks = D // width

    def one_block(packed):
        sig_block, query_block, rate_block, res_block, skip_block = packed
        lag_pos = jnp.arange(WINDOW, dtype=jnp.float32)
        filt = lax.optimization_barrier(jnp.sum(res_block[:, :, None] * jnp.exp(-rate_block[:, :, None] * lag_pos), axis=0))
        signal = sig_block.astype(jnp.float32)
        length = 2 * WINDOW
        spectrum = jnp.fft.rfft(signal, length) * jnp.fft.rfft(filt, length)[None]
        conv = jnp.fft.irfft(spectrum, length)[..., :WINDOW]
        conv = conv + skip_block[None, :, None] * signal
        mixed_block = (query_block.astype(jnp.float32) * conv).astype(jnp.bfloat16)
        weights = jnp.exp(-rate_block[:, :, None] * (WINDOW - 1 - lag_pos))
        state_block = jnp.einsum('mcl,bcl->bmc', weights, signal, precision=highest)
        return (mixed_block, state_block)
    packed = (product.reshape(BATCH, nblocks, width, WINDOW).transpose(1, 0, 2, 3), query.reshape(BATCH, nblocks, width, WINDOW).transpose(1, 0, 2, 3), decay_rate.reshape(MODES, nblocks, width).transpose(1, 0, 2), residue.reshape(MODES, nblocks, width).transpose(1, 0, 2), skip_weight.reshape(nblocks, width))
    mixed_blocks, state_blocks = lax.map(one_block, packed)
    mixed = mixed_blocks.transpose(1, 0, 2, 3).reshape(BATCH, D, WINDOW)
    state = state_blocks.transpose(1, 2, 0, 3).reshape(BATCH, MODES, D)
    embedded = jnp.take(embedding, tokens, axis=0).astype(jnp.float32)
    mean_sq = lax.optimization_barrier(jnp.sum(embedded * embedded, axis=-1, keepdims=True)) / D
    normed = (embedded * lax.rsqrt(mean_sq + 1e-05) * norm_gain).astype(jnp.bfloat16)
    proj = jnp.einsum('bsd,idc->ibsc', normed.astype(jnp.float32), dec_weight.astype(jnp.float32)).astype(jnp.bfloat16)
    decay = jnp.exp(-decay_rate)
    running = state
    outputs = []
    for step in range(STEPS):
        rounded = lax.optimization_barrier((proj[1, :, step].astype(jnp.float32) * proj[2, :, step].astype(jnp.float32)).astype(jnp.bfloat16))
        mixed_in = rounded.astype(jnp.float32)
        running = decay[None] * running + mixed_in[:, None, :]
        conv_step = lax.optimization_barrier(jnp.sum(residue[None] * running, axis=1)) + skip_weight[None] * mixed_in
        outputs.append((proj[0, :, step].astype(jnp.float32) * conv_step).astype(jnp.bfloat16))
    decode_mix = jnp.stack(outputs, axis=1)
    decoded = jnp.dot(decode_mix.reshape(BATCH * STEPS, D), out_weight, preferred_element_type=jnp.float32)
    decoded = decoded.astype(jnp.bfloat16).reshape(BATCH, STEPS, D)
    return (mixed, decoded)
```

```python
import jax
import jax.numpy as jnp
from jax import lax
from jax.experimental import pallas as pl
from jax.experimental.pallas import tpu as pltpu
from jax.sharding import PartitionSpec as P

LANES = 128
SUB = 8
EPS = 1e-05


def quarter_of(shape):
    return lax.broadcasted_iota(jnp.int32, shape, len(shape) - 1) // 32


def spread(tiles, sign):
    quarter = quarter_of((SUB, LANES))
    made = []
    for q in range(4):
        total = None
        for r in range(4):
            shift = (32 * (r - q)) % LANES
            moved = tiles[r] if shift == 0 else pltpu.roll(tiles[r], shift, 1)
            total = moved if total is None else jnp.where(quarter == r, moved, total)
        made.append(total)
    return made


def rounded(x):
    return x.astype(jnp.bfloat16).astype(jnp.float32)


def first_kernel(modes, shard, tokens, offsets, k_ref, v_ref, rate_ref, emb_ref, gain_ref, w_ref,
                 u_out, send, trans, decay, state, x16, squares):
    half = pl.program_id(0)
    position = lax.axis_index("seq") * shard + lax.broadcasted_iota(jnp.int32, (LANES, shard), 1)
    batch = k_ref.shape[1]
    steps = tokens.shape[1]
    count = batch * steps

    @pl.when(half == 0)
    def _():
        vocab = emb_ref.shape[0]
        row = lax.broadcasted_iota(jnp.int32, (16, vocab), 0)
        wanted = jnp.full((16, vocab), -1, jnp.int32)
        for t in range(count):
            wanted = jnp.where(row == t, tokens[t // steps, t % steps], wanted)
        hot = (lax.broadcasted_iota(jnp.int32, (16, vocab), 1) == wanted).astype(jnp.float32)
        x = jnp.dot(hot.astype(jnp.bfloat16), emb_ref[...], preferred_element_type=jnp.float32)[:SUB]
        squares[...] = jnp.broadcast_to(jnp.sum(x * x, axis=1, keepdims=True), (SUB, LANES))
        scaled = x * gain_ref[...]
        high = rounded(scaled)
        x16[...] = jnp.concatenate([high, scaled - high], axis=0).astype(jnp.bfloat16)

    for g in range(SUB):
        decay[pl.ds(g, modes, stride=SUB), :] = jnp.exp(-rate_ref[:, g * LANES:(g + 1) * LANES])
        for b in range(batch):
            rows = slice(g * LANES, (g + 1) * LANES)
            product = k_ref[0, b, rows].astype(jnp.float32) * v_ref[0, b, rows].astype(jnp.float32)
            u = rounded(jnp.where(position >= offsets[b], product, 0.0))
            trans[pl.ds((b * SUB + g) * shard, shard), :] = u.T

    rates = [decay[m * SUB:(m + 1) * SUB, :] for m in range(modes)]

    def step(t, held):
        held = list(held)
        for b in range(batch):
            u = trans[pl.ds(b * SUB * shard + t, SUB, stride=shard), :]
            u_out[0, b, t] = u
            for m in range(modes):
                at = b * modes + m
                held[at] = rates[m] * held[at] + u
        return tuple(held)

    zero = jnp.zeros((SUB, LANES), jnp.float32)
    held = lax.fori_loop(0, shard, step, (zero,) * (batch * modes), unroll=2)
    for at in range(batch * modes):
        state[at * SUB:(at + 1) * SUB, :] = held[at]

    terms = []
    for i in range(3):
        both = jnp.dot(x16[...], w_ref[i], preferred_element_type=jnp.float32)
        terms.append(both[:SUB] + both[SUB:])
    for g in range(SUB):
        ends = spread([state[pl.ds(g + r * 64, SUB, stride=SUB), :] for r in range(4)], 1)
        parts = spread([t[:, g * LANES:(g + 1) * LANES] for t in terms] + [squares[...]], 1)
        for q in range(4):
            send[g * 4 + q, :SUB] = ends[q]
            send[g * 4 + q, SUB:] = parts[q]


def owner_kernel(width, shard, steps, got, rate_ref, res_ref, skip_ref, back):
    owner = lax.axis_index("seq")
    group, part = owner // 4, owner % 4
    turn = (LANES - 32 * part) % LANES
    quarter = quarter_of((SUB, LANES))

    def four(a, b, c, d):
        b, c, d = pltpu.roll(b, 32, 1), pltpu.roll(c, 64, 1), pltpu.roll(d, 96, 1)
        return jnp.where(quarter == 0, a, jnp.where(quarter == 1, b, jnp.where(quarter == 2, c, d)))

    def packed(ref):
        own = ref[:, pl.ds(pl.multiple_of(group * LANES, LANES), LANES)]
        own = pltpu.roll(own, turn, 1)
        low, high = own[:SUB], own[SUB:]
        return four(low, high, low, high)

    rate = packed(rate_ref)
    res = packed(res_ref)
    jump = jnp.exp(-rate * shard)
    carried = jnp.zeros((SUB, LANES), jnp.float32)
    total = jnp.zeros((SUB, LANES), jnp.float32)
    for i in range(got.shape[0]):
        back[i, :SUB] = carried
        carried = jump * carried + got[i, :SUB]
        total = total + got[i, SUB:]
    scale = lax.rsqrt(pltpu.roll(total, 32, 1) / width + EPS)
    query = rounded(total * scale)
    key = rounded(pltpu.roll(total, 96, 1) * scale)
    value = rounded(pltpu.roll(total, 64, 1) * scale)
    weight = rounded(key * value)
    weight = four(weight, weight, weight, weight)
    skip = jnp.broadcast_to(skip_ref[pl.ds(group, 1), :], (SUB, LANES))
    skip = pltpu.roll(skip, turn, 1)
    skip = four(skip, skip, skip, skip)
    decay = jnp.exp(-rate)
    row = lax.broadcasted_iota(jnp.int32, (SUB, LANES), 0)
    conv = jnp.zeros((SUB, LANES), jnp.float32)
    for s in range(steps):
        first = jnp.broadcast_to(weight[s:s + 1], (SUB, LANES))
        second = jnp.broadcast_to(weight[steps + s:steps + s + 1], (SUB, LANES))
        w = jnp.where(quarter < 2, first, second)
        carried = decay * carried + w
        summed = jnp.broadcast_to(jnp.sum(res * carried, axis=0, keepdims=True), (SUB, LANES))
        summed = summed + pltpu.roll(summed, 96, 1) + skip * w
        conv = jnp.where(row == s, summed, conv)
        conv = jnp.where(row == steps + s, pltpu.roll(summed, 64, 1), conv)
    mix = rounded(query * conv)
    for i in range(got.shape[0]):
        back[i, SUB:] = mix


def decode_kernel(mix_ref, w_ref, out):
    quarter = quarter_of((SUB, LANES))
    pieces = []
    for g in range(mix_ref.shape[0] // 4):
        tile = mix_ref[g * 4]
        for q in range(1, 4):
            tile = jnp.where(quarter == q, pltpu.roll(mix_ref[g * 4 + q], 32 * q, 1), tile)
        pieces.append(tile)
    mix = jnp.concatenate(pieces, axis=1).astype(jnp.bfloat16)
    summed = jnp.dot(mix, w_ref[...], preferred_element_type=jnp.float32)
    for k in range(4):
        out[k] = summed[:, k * 32:(k + 1) * 32]


def last_kernel(modes, shard, carry_ref, u_ref, q_ref, rate_ref, res_ref, skip_ref,
                out, trans, decay, weight, state):
    batch = u_ref.shape[1]
    for g in range(SUB):
        lanes = slice(g * LANES, (g + 1) * LANES)
        decay[pl.ds(g, modes, stride=SUB), :] = jnp.exp(-rate_ref[:, lanes])
        weight[pl.ds(g, modes, stride=SUB), :] = res_ref[:, lanes]
        tiles = spread([carry_ref[g * 4 + q] for q in range(4)], 1)
        for r in range(4):
            state[pl.ds(g + r * 64, SUB, stride=SUB), :] = tiles[r]
    rates = [decay[m * SUB:(m + 1) * SUB, :] for m in range(modes)]
    weights = [weight[m * SUB:(m + 1) * SUB, :] for m in range(modes)]
    skip = skip_ref[...]
    for b in range(batch):
        def step(t, held):
            held = list(held)
            u = u_ref[0, b, t]
            terms = [skip * u]
            for m in range(modes):
                held[m] = rates[m] * held[m] + u
                terms.append(weights[m] * held[m])
            while len(terms) > 1:
                terms = [x + y for x, y in zip(terms[::2], terms[1::2])] + terms[len(terms) // 2 * 2:]
            trans[pl.ds(t, SUB, stride=shard), :] = terms[0]
            return tuple(held)

        held = tuple(state[(b * modes + m) * SUB:(b * modes + m + 1) * SUB, :] for m in range(modes))
        lax.fori_loop(0, shard, step, held, unroll=2)
        for g in range(SUB):
            rows = slice(g * LANES, (g + 1) * LANES)
            conv = trans[pl.ds(g * shard, shard), :].T
            out[b, rows] = (q_ref[0, b, rows].astype(jnp.float32) * conv).astype(jnp.bfloat16)


def body(features, offsets, tokens, decay_rate, residue, skip_weight, embedding, norm_gain, dec_weight, out_weight):
    _, batch, chans, shard = features.shape
    modes = decay_rate.shape[0]
    steps = tokens.shape[1]
    vocab = embedding.shape[0]
    devices = lax.axis_size("seq")
    width = devices * norm_gain.shape[0]
    block = SUB * LANES
    halves = chans // block
    f32 = jnp.float32
    gain = norm_gain.reshape(1, -1)
    skip = skip_weight.reshape(chans // LANES, LANES)

    u_t, send = pl.pallas_call(
        lambda *refs: first_kernel(modes, shard, *refs),
        grid_spec=pltpu.PrefetchScalarGridSpec(
            num_scalar_prefetch=2,
            grid=(halves,),
            in_specs=[
                pl.BlockSpec((1, batch, block, shard), lambda h, *_: (1, 0, h, 0)),
                pl.BlockSpec((1, batch, block, shard), lambda h, *_: (2, 0, h, 0)),
                pl.BlockSpec((modes, block), lambda h, *_: (0, h)),
                pl.BlockSpec((vocab, shard), lambda h, *_: (0, 0)),
                pl.BlockSpec((1, shard), lambda h, *_: (0, 0)),
                pl.BlockSpec((3, shard, block), lambda h, *_: (0, 0, h)),
            ],
            out_specs=[
                pl.BlockSpec((1, batch, shard, SUB, LANES), lambda h, *_: (h, 0, 0, 0, 0)),
                pl.BlockSpec((devices // halves, 2 * SUB, LANES), lambda h, *_: (h, 0, 0)),
            ],
            scratch_shapes=[
                pltpu.VMEM((batch * SUB * shard, LANES), f32),
                pltpu.VMEM((modes * SUB, LANES), f32),
                pltpu.VMEM((batch * modes * SUB, LANES), f32),
                pltpu.VMEM((16, shard), jnp.bfloat16),
                pltpu.VMEM((SUB, LANES), f32),
            ],
        ),
        out_shape=[
            jax.ShapeDtypeStruct((halves, batch, shard, SUB, LANES), f32),
            jax.ShapeDtypeStruct((devices, 2 * SUB, LANES), f32),
        ],
        name="first",
    )(tokens, offsets, features, features, decay_rate, embedding, gain, dec_weight)

    got = lax.all_to_all(send, "seq", split_axis=0, concat_axis=0, tiled=True)

    back = pl.pallas_call(
        lambda *refs: owner_kernel(width, shard, steps, *refs),
        out_shape=jax.ShapeDtypeStruct((devices, 2 * SUB, LANES), f32),
        name="owner",
    )(got, decay_rate, residue, skip)

    given = lax.all_to_all(back, "seq", split_axis=0, concat_axis=0, tiled=True)

    partial = pl.pallas_call(
        decode_kernel,
        grid=(1,),
        in_specs=[
            pl.BlockSpec((devices, SUB, LANES), lambda i: (0, 1, 0)),
            pl.BlockSpec((chans, LANES), lambda i: (0, 0)),
        ],
        out_specs=pl.BlockSpec((4, SUB, 32), lambda i: (0, 0, 0)),
        out_shape=jax.ShapeDtypeStruct((4, SUB, 32), f32),
        name="decode",
    )(given, out_weight)
    pieces = lax.all_to_all(partial, "chan", split_axis=0, concat_axis=0, tiled=True)
    decoded = jnp.sum(pieces, axis=0).astype(jnp.bfloat16).reshape(batch, steps, 32)

    mixed = pl.pallas_call(
        lambda *refs: last_kernel(modes, shard, *refs),
        grid=(halves,),
        in_specs=[
            pl.BlockSpec((devices // halves, SUB, LANES), lambda h: (h, 0, 0)),
            pl.BlockSpec((1, batch, shard, SUB, LANES), lambda h: (h, 0, 0, 0, 0)),
            pl.BlockSpec((1, batch, block, shard), lambda h: (0, 0, h, 0)),
            pl.BlockSpec((modes, block), lambda h: (0, h)),
            pl.BlockSpec((modes, block), lambda h: (0, h)),
            pl.BlockSpec((SUB, LANES), lambda h: (h, 0)),
        ],
        out_specs=pl.BlockSpec((batch, block, shard), lambda h: (0, h, 0)),
        out_shape=jax.ShapeDtypeStruct((batch, chans, shard), jnp.bfloat16),
        scratch_shapes=[
            pltpu.VMEM((SUB * shard, LANES), f32),
            pltpu.VMEM((modes * SUB, LANES), f32),
            pltpu.VMEM((modes * SUB, LANES), f32),
            pltpu.VMEM((batch * modes * SUB, LANES), f32),
        ],
        cost_estimate=pl.CostEstimate(flops=2**25, bytes_accessed=2**22, transcendentals=0),
        name="last",
    )(given, u_t, features, decay_rate, residue, skip)
    return (mixed, decoded)


def solution(mesh):
    placed = (
        P(None, None, "chan", "seq"),
        P(),
        P(),
        P(None, "chan"),
        P(None, "chan"),
        P("chan"),
        P(None, "seq"),
        P("seq"),
        P(None, "seq", "chan"),
        P("chan", "seq"),
    )
    return jax.shard_map(
        body,
        mesh=mesh,
        in_specs=placed,
        out_specs=(P(None, "chan", "seq"), P(None, None, ("seq", "chan"))),
        check_vma=False,
    )
```

```python
import jax
import jax.numpy as jnp
from jax import lax
from jax.experimental import pallas as pl
from jax.experimental.pallas import tpu as pltpu
from jax.sharding import PartitionSpec as P

LANES = 128
SUB = 8
GROUPS = 4
PAD = 9
PITCH = 132
EPS = 1e-05
VMEM_LIMIT = 8 * 2**20
WIDE_LIMIT = 60 * 2**20


def quarter_of(shape):
    return lax.broadcasted_iota(jnp.int32, shape, len(shape) - 1) // 32


def spread(tiles):
    lane = lax.broadcasted_iota(jnp.int32, tiles[0].shape, 1)
    low, even = lane < 64, (lane // 32) % 2 == 0
    made = list(tiles)
    for r in range(2):
        a, b = tiles[r], tiles[r + 2]
        made[r] = jnp.where(low, a, pltpu.roll(b, 64, 1))
        made[r + 2] = jnp.where(low, pltpu.roll(a, 64, 1), b)
    for r in (0, 2):
        a, b = made[r], made[r + 1]
        made[r] = jnp.where(even, a, pltpu.roll(b, 32, 1))
        made[r + 1] = jnp.where(even, pltpu.roll(a, 96, 1), b)
    return made


def rounded(x):
    return x.astype(jnp.bfloat16).astype(jnp.float32)


def pairs_sum(terms):
    while len(terms) > 1:
        terms = [x + y for x, y in zip(terms[::2], terms[1::2])] + terms[len(terms) // 2 * 2:]
    return terms[0]


def fill(scratch, ref, batch, fn):
    modes = ref.shape[0]
    for g in range(GROUPS):
        values = fn(ref[:, g * LANES:(g + 1) * LANES])
        for b in range(batch):
            scratch[pl.ds(b * GROUPS + g, modes, stride=PAD), :] = values


def tiles_of(scratch, modes):
    return [scratch[m * PAD:m * PAD + SUB, :] for m in range(modes)]


def first_kernel(modes, shard, tokens, offsets, k_ref, v_ref, rate_ref, emb_ref, gain_ref, w_ref,
                 u_out, send, trans, decay, state, x16, squares):
    part = pl.program_id(0)
    position = lax.axis_index("seq") * shard + lax.broadcasted_iota(jnp.int32, (LANES, shard), 1)
    batch = k_ref.shape[1]
    steps = tokens.shape[1]
    count = batch * steps

    @pl.when(part == 0)
    def _():
        vocab = emb_ref.shape[0]
        row = lax.broadcasted_iota(jnp.int32, (16, vocab), 0)
        wanted = jnp.full((16, vocab), -1, jnp.int32)
        for t in range(count):
            wanted = jnp.where(row == t, tokens[t // steps, t % steps], wanted)
        hot = (lax.broadcasted_iota(jnp.int32, (16, vocab), 1) == wanted).astype(jnp.float32)
        x = jnp.dot(hot.astype(jnp.bfloat16), emb_ref[...], preferred_element_type=jnp.float32)[:SUB]
        squares[...] = jnp.broadcast_to(jnp.sum(x * x, axis=1, keepdims=True), (SUB, LANES))
        scaled = x * gain_ref[...]
        high = rounded(scaled)
        x16[...] = jnp.concatenate([high, scaled - high], axis=0).astype(jnp.bfloat16)

    fill(decay, rate_ref, batch, lambda x: jnp.exp(-x))
    for g in range(GROUPS):
        for b in range(batch):
            rows = slice(g * LANES, (g + 1) * LANES)
            product = k_ref[0, b, rows].astype(jnp.float32) * v_ref[0, b, rows].astype(jnp.float32)
            u = rounded(jnp.where(position >= offsets[b], product, 0.0))
            trans[pl.ds((b * GROUPS + g) * PITCH, shard), :] = u.T

    rates = tiles_of(decay, modes)

    def step(t, held):
        u = trans[pl.ds(t, SUB, stride=PITCH), :]
        u_out[0, t] = u
        return tuple(rates[m] * held[m] + u for m in range(modes))

    zero = jnp.zeros((SUB, LANES), jnp.float32)
    held = lax.fori_loop(0, shard, step, (zero,) * modes, unroll=4)
    for m in range(modes):
        state[m * PAD:m * PAD + SUB, :] = held[m]

    terms = []
    for i in range(3):
        both = jnp.dot(x16[...], w_ref[i], preferred_element_type=jnp.float32)
        terms.append(both[:SUB] + both[SUB:])
    for g in range(GROUPS):
        ends = [state[pl.ds((r // 2) * GROUPS + g + (r % 2) * SUB * PAD, SUB, stride=PAD), :] for r in range(4)]
        ends = spread(ends)
        parts = spread([t[:, g * LANES:(g + 1) * LANES] for t in terms] + [squares[...]])
        for q in range(4):
            send[g * 4 + q, :SUB] = ends[q]
            send[g * 4 + q, SUB:] = parts[q]


def local_kernel(modes, shard, u_ref, rate_ref, res_ref, skip_ref, out, decay, weight):
    batch = SUB // GROUPS
    fill(decay, rate_ref, batch, lambda x: jnp.exp(-x))
    fill(weight, res_ref, batch, lambda x: x)
    rates, weights = tiles_of(decay, modes), tiles_of(weight, modes)
    skip = jnp.concatenate([skip_ref[0]] * batch, axis=0)

    def step(t, held):
        u = u_ref[0, t]
        held = tuple(rates[m] * held[m] + u for m in range(modes))
        out[0, t] = pairs_sum([weights[m] * held[m] for m in range(modes)] + [skip * u])
        return held

    zero = jnp.zeros((SUB, LANES), jnp.float32)
    lax.fori_loop(0, shard, step, (zero,) * modes, unroll=2)


def owner_kernel(width, shard, steps, got, rate_ref, res_ref, skip_ref, back):
    owner = lax.axis_index("seq")
    group, part = owner // 4, owner % 4
    turn = (LANES - 32 * part) % LANES
    quarter = quarter_of((SUB, LANES))

    def four(a, b, c, d):
        b, c, d = pltpu.roll(b, 32, 1), pltpu.roll(c, 64, 1), pltpu.roll(d, 96, 1)
        return jnp.where(quarter == 0, a, jnp.where(quarter == 1, b, jnp.where(quarter == 2, c, d)))

    def packed(ref):
        own = ref[:, pl.ds(pl.multiple_of(group * LANES, LANES), LANES)]
        own = pltpu.roll(own, turn, 1)
        low, high = own[:SUB], own[SUB:]
        return four(low, high, low, high)

    rate = packed(rate_ref)
    res = packed(res_ref)
    jump = jnp.exp(-rate * shard)
    carried = jnp.zeros((SUB, LANES), jnp.float32)
    total = jnp.zeros((SUB, LANES), jnp.float32)
    for i in range(got.shape[0]):
        back[i, :SUB] = carried
        carried = jump * carried + got[i, :SUB]
        total = total + got[i, SUB:]
    scale = lax.rsqrt(pltpu.roll(total, 32, 1) / width + EPS)
    query = rounded(total * scale)
    key = rounded(pltpu.roll(total, 96, 1) * scale)
    value = rounded(pltpu.roll(total, 64, 1) * scale)
    weight = rounded(key * value)
    weight = four(weight, weight, weight, weight)
    skip = jnp.broadcast_to(skip_ref[pl.ds(group, 1), :], (SUB, LANES))
    skip = pltpu.roll(skip, turn, 1)
    skip = four(skip, skip, skip, skip)
    decay = jnp.exp(-rate)
    row = lax.broadcasted_iota(jnp.int32, (SUB, LANES), 0)
    conv = jnp.zeros((SUB, LANES), jnp.float32)
    for s in range(steps):
        first = jnp.broadcast_to(weight[s:s + 1], (SUB, LANES))
        second = jnp.broadcast_to(weight[steps + s:steps + s + 1], (SUB, LANES))
        w = jnp.where(quarter < 2, first, second)
        carried = decay * carried + w
        summed = jnp.broadcast_to(jnp.sum(res * carried, axis=0, keepdims=True), (SUB, LANES))
        summed = summed + pltpu.roll(summed, 96, 1) + skip * w
        conv = jnp.where(row == s, summed, conv)
        conv = jnp.where(row == steps + s, pltpu.roll(summed, 64, 1), conv)
    mix = rounded(query * conv)
    for i in range(got.shape[0]):
        back[i, SUB:] = mix


def decode_kernel(steps, mix_ref, w_ref, out):
    quarter = quarter_of((SUB, LANES))
    pieces = []
    for g in range(mix_ref.shape[0] // 4):
        tile = mix_ref[g * 4]
        for q in range(1, 4):
            tile = jnp.where(quarter == q, pltpu.roll(mix_ref[g * 4 + q], 32 * q, 1), tile)
        pieces.append(tile)
    mix = jnp.concatenate(pieces, axis=1).astype(jnp.bfloat16)
    summed = jnp.dot(mix, w_ref[...], preferred_element_type=jnp.float32)
    rows = SUB // steps
    ordered = [jnp.concatenate([summed[b * steps + s:b * steps + s + 1] for b in range(rows)], axis=0) for s in range(steps)]
    for k, tile in enumerate(spread(ordered)):
        out[k] = tile


def finish_kernel(steps, ref, out):
    total = ref[0] + ref[1] + ref[2] + ref[3]
    for s in range(steps):
        out[:, s, :] = total[:, s * 32:(s + 1) * 32].astype(jnp.bfloat16)


def last_kernel(modes, shard, carry_ref, near_ref, q_ref, rate_ref, res_ref, out, trans, decay, weight, state):
    batch = q_ref.shape[1]
    fill(decay, rate_ref, batch, lambda x: jnp.exp(-x))
    fill(weight, res_ref, batch, lambda x: x)
    for g in range(GROUPS):
        tiles = spread([carry_ref[g * 4 + q] for q in range(4)])
        for r in range(4):
            state[pl.ds((r // 2) * GROUPS + g + (r % 2) * SUB * PAD, SUB, stride=PAD), :] = tiles[r]
    rates, weights = tiles_of(decay, modes), tiles_of(weight, modes)

    def step(t, held):
        trans[pl.ds(t, SUB, stride=PITCH), :] = pairs_sum(list(held) + [near_ref[0, t]])
        return tuple(rates[m] * held[m] for m in range(modes))

    held = tuple(weights[m] * (rates[m] * state[m * PAD:m * PAD + SUB, :]) for m in range(modes))
    lax.fori_loop(0, shard, step, held, unroll=4)
    for b in range(batch):
        for g in range(GROUPS):
            rows = slice(g * LANES, (g + 1) * LANES)
            conv = trans[pl.ds((b * GROUPS + g) * PITCH, shard), :].T
            out[b, rows] = (q_ref[0, b, rows].astype(jnp.float32) * conv).astype(jnp.bfloat16)


def body(features, offsets, tokens, decay_rate, residue, skip_weight, embedding, norm_gain, dec_weight, out_weight):
    _, batch, chans, shard = features.shape
    modes = decay_rate.shape[0]
    steps = tokens.shape[1]
    vocab = embedding.shape[0]
    devices = lax.axis_size("seq")
    width = devices * norm_gain.shape[0]
    block = GROUPS * LANES
    parts = chans // block
    f32 = jnp.float32
    gain = norm_gain.reshape(1, -1)
    skip = skip_weight.reshape(chans // LANES, LANES)
    per_mode = pltpu.VMEM((modes * PAD, LANES), f32)
    across = pltpu.VMEM((SUB * PITCH, LANES), f32)
    by_part = pl.BlockSpec((modes, block), lambda h, *_: (0, h))
    in_time = pl.BlockSpec((1, shard, SUB, LANES), lambda h, *_: (h, 0, 0, 0))
    wide = pltpu.CompilerParams(vmem_limit_bytes=WIDE_LIMIT)
    limit = pltpu.CompilerParams(vmem_limit_bytes=VMEM_LIMIT)

    u_t, send = pl.pallas_call(
        lambda *refs: first_kernel(modes, shard, *refs),
        grid_spec=pltpu.PrefetchScalarGridSpec(
            num_scalar_prefetch=2,
            grid=(parts,),
            in_specs=[
                pl.BlockSpec((1, batch, block, shard), lambda h, *_: (1, 0, h, 0)),
                pl.BlockSpec((1, batch, block, shard), lambda h, *_: (2, 0, h, 0)),
                by_part,
                pl.BlockSpec((vocab, shard), lambda h, *_: (0, 0)),
                pl.BlockSpec((1, shard), lambda h, *_: (0, 0)),
                pl.BlockSpec((3, shard, block), lambda h, *_: (0, 0, h)),
            ],
            out_specs=[in_time, pl.BlockSpec((devices // parts, 2 * SUB, LANES), lambda h, *_: (h, 0, 0))],
            scratch_shapes=[across, per_mode, per_mode, pltpu.VMEM((16, shard), jnp.bfloat16), pltpu.VMEM((SUB, LANES), f32)],
        ),
        out_shape=[
            jax.ShapeDtypeStruct((parts, shard, SUB, LANES), f32),
            jax.ShapeDtypeStruct((devices, 2 * SUB, LANES), f32),
        ],
        compiler_params=wide,
        name="first",
    )(tokens, offsets, features, features, decay_rate, embedding, gain, dec_weight)

    got = lax.all_to_all(send, "seq", split_axis=0, concat_axis=0, tiled=True)

    near = pl.pallas_call(
        lambda *refs: local_kernel(modes, shard, *refs),
        grid=(parts,),
        in_specs=[in_time, by_part, by_part, pl.BlockSpec((1, GROUPS, LANES), lambda h: (h, 0, 0))],
        out_specs=in_time,
        out_shape=jax.ShapeDtypeStruct((parts, shard, SUB, LANES), f32),
        scratch_shapes=[per_mode, per_mode],
        compiler_params=wide,
        cost_estimate=pl.CostEstimate(flops=2**25, bytes_accessed=2**22, transcendentals=0),
        name="local",
    )(u_t, decay_rate, residue, skip.reshape(parts, GROUPS, LANES))

    got, near = lax.optimization_barrier((got, near))
    back = pl.pallas_call(
        lambda *refs: owner_kernel(width, shard, steps, *refs),
        out_shape=jax.ShapeDtypeStruct((devices, 2 * SUB, LANES), f32),
        compiler_params=limit,
        name="owner",
    )(got, decay_rate, residue, skip)

    given = lax.all_to_all(back, "seq", split_axis=0, concat_axis=0, tiled=True)

    partial = pl.pallas_call(
        lambda *refs: decode_kernel(steps, *refs),
        grid=(1,),
        in_specs=[
            pl.BlockSpec((devices, SUB, LANES), lambda i: (0, 1, 0)),
            pl.BlockSpec((chans, LANES), lambda i: (0, 0)),
        ],
        out_specs=pl.BlockSpec((4, batch, LANES), lambda i: (0, 0, 0)),
        out_shape=jax.ShapeDtypeStruct((4, batch, LANES), f32),
        compiler_params=limit,
        name="decode",
    )(given, out_weight)
    pieces = lax.all_to_all(partial, "chan", split_axis=0, concat_axis=0, tiled=True)

    mixed = pl.pallas_call(
        lambda *refs: last_kernel(modes, shard, *refs),
        grid=(parts,),
        in_specs=[
            pl.BlockSpec((devices // parts, SUB, LANES), lambda h: (h, 0, 0)),
            in_time,
            pl.BlockSpec((1, batch, block, shard), lambda h: (0, 0, h, 0)),
            by_part,
            by_part,
        ],
        out_specs=pl.BlockSpec((batch, block, shard), lambda h: (0, h, 0)),
        out_shape=jax.ShapeDtypeStruct((batch, chans, shard), jnp.bfloat16),
        scratch_shapes=[across, per_mode, per_mode, per_mode],
        compiler_params=wide,
        cost_estimate=pl.CostEstimate(flops=2**25, bytes_accessed=2**22, transcendentals=0),
        name="last",
    )(given, near, features, decay_rate, residue)

    decoded = pl.pallas_call(
        lambda *refs: finish_kernel(steps, *refs),
        out_shape=jax.ShapeDtypeStruct((batch, steps, 32), jnp.bfloat16),
        compiler_params=limit,
        name="finish",
    )(pieces)
    return (mixed, decoded)


def solution(mesh):
    placed = (
        P(None, None, "chan", "seq"),
        P(),
        P(),
        P(None, "chan"),
        P(None, "chan"),
        P("chan"),
        P(None, "seq"),
        P("seq"),
        P(None, "seq", "chan"),
        P("chan", "seq"),
    )
    return jax.shard_map(
        body,
        mesh=mesh,
        in_specs=placed,
        out_specs=(P(None, "chan", "seq"), P(None, None, ("seq", "chan"))),
        check_vma=False,
    )
```

```python
import jax
import jax.numpy as jnp
from jax import lax
from jax.experimental import pallas as pl
from jax.experimental.pallas import tpu as pltpu
from jax.sharding import PartitionSpec as P

LANES = 128
SUB = 8
GROUPS = 4
PAD = 9
PITCH = 132
EPS = 1e-05
VMEM_LIMIT = 8 * 2**20
WIDE_LIMIT = 60 * 2**20


def quarter_of(shape):
    return lax.broadcasted_iota(jnp.int32, shape, len(shape) - 1) // 32


def spread(tiles):
    lane = lax.broadcasted_iota(jnp.int32, tiles[0].shape, 1)
    low, even = lane < 64, (lane // 32) % 2 == 0
    made = list(tiles)
    for r in range(2):
        a, b = tiles[r], tiles[r + 2]
        made[r] = jnp.where(low, a, pltpu.roll(b, 64, 1))
        made[r + 2] = jnp.where(low, pltpu.roll(a, 64, 1), b)
    for r in (0, 2):
        a, b = made[r], made[r + 1]
        made[r] = jnp.where(even, a, pltpu.roll(b, 32, 1))
        made[r + 1] = jnp.where(even, pltpu.roll(a, 96, 1), b)
    return made


def rounded(x):
    return x.astype(jnp.bfloat16).astype(jnp.float32)


def pairs_sum(terms):
    while len(terms) > 1:
        terms = [x + y for x, y in zip(terms[::2], terms[1::2])] + terms[len(terms) // 2 * 2:]
    return terms[0]


def fill(scratch, ref, batch, fn):
    modes = ref.shape[0]
    for g in range(GROUPS):
        values = fn(ref[:, g * LANES:(g + 1) * LANES])
        for b in range(batch):
            scratch[pl.ds(b * GROUPS + g, modes, stride=PAD), :] = values


def tiles_of(scratch, modes):
    return [scratch[m * PAD:m * PAD + SUB, :] for m in range(modes)]


def first_kernel(modes, shard, tokens, offsets, k_ref, v_ref, rate_ref, emb_ref, gain_ref, w_ref,
                 u_out, send, trans, decay, state, x16, squares, sums):
    part = pl.program_id(0)
    position = lax.axis_index("seq") * shard + lax.broadcasted_iota(jnp.int32, (LANES, shard), 1)
    batch = k_ref.shape[1]
    steps = tokens.shape[1]
    count = batch * steps

    @pl.when(part == 0)
    def _():
        vocab = emb_ref.shape[0]
        row = lax.broadcasted_iota(jnp.int32, (16, vocab), 0)
        wanted = jnp.full((16, vocab), -1, jnp.int32)
        for t in range(count):
            wanted = jnp.where(row == t, tokens[t // steps, t % steps], wanted)
        hot = (lax.broadcasted_iota(jnp.int32, (16, vocab), 1) == wanted).astype(jnp.float32)
        x = jnp.dot(hot.astype(jnp.bfloat16), emb_ref[...], preferred_element_type=jnp.float32)[:SUB]
        squares[...] = jnp.broadcast_to(jnp.sum(x * x, axis=1, keepdims=True), (SUB, LANES))
        scaled = x * gain_ref[...]
        high = rounded(scaled)
        x16[...] = jnp.concatenate([high, scaled - high], axis=0).astype(jnp.bfloat16)

    fill(decay, rate_ref, batch, lambda x: jnp.exp(-x))
    for g in range(GROUPS):
        for b in range(batch):
            rows = slice(g * LANES, (g + 1) * LANES)
            product = k_ref[0, b, rows].astype(jnp.float32) * v_ref[0, b, rows].astype(jnp.float32)
            u = rounded(jnp.where(position >= offsets[b], product, 0.0))
            trans[pl.ds((b * GROUPS + g) * PITCH, shard), :] = u.T

    terms = []
    for i in range(3):
        both = jnp.dot(x16[...], w_ref[i], preferred_element_type=jnp.float32)
        terms.append(both[:SUB] + both[SUB:])
    for g in range(GROUPS):
        parts = spread([t[:, g * LANES:(g + 1) * LANES] for t in terms] + [squares[...]])
        for q in range(4):
            sums[g * 4 + q] = parts[q]

    rates = tiles_of(decay, modes)

    def step(t, held):
        u = trans[pl.ds(t, SUB, stride=PITCH), :]
        u_out[0, t] = u
        return tuple(rates[m] * held[m] + u for m in range(modes))

    zero = jnp.zeros((SUB, LANES), jnp.float32)
    held = lax.fori_loop(0, shard, step, (zero,) * modes, unroll=4)
    for m in range(modes):
        state[m * PAD:m * PAD + SUB, :] = held[m]

    for g in range(GROUPS):
        ends = [state[pl.ds((r // 2) * GROUPS + g + (r % 2) * SUB * PAD, SUB, stride=PAD), :] for r in range(4)]
        for q, tile in enumerate(spread(ends)):
            send[g * 4 + q] = jnp.concatenate([tile, sums[g * 4 + q]], axis=0).astype(jnp.bfloat16)


def local_kernel(modes, shard, u_ref, rate_ref, res_ref, skip_ref, out, decay, weight):
    batch = SUB // GROUPS
    fill(decay, rate_ref, batch, lambda x: jnp.exp(-x))
    fill(weight, res_ref, batch, lambda x: x)
    rates, weights = tiles_of(decay, modes), tiles_of(weight, modes)
    skip = jnp.concatenate([skip_ref[0]] * batch, axis=0)

    def step(t, held):
        u = u_ref[0, t]
        held = tuple(rates[m] * held[m] + u for m in range(modes))
        out[0, t] = pairs_sum([weights[m] * held[m] for m in range(modes)] + [skip * u])
        return held

    zero = jnp.zeros((SUB, LANES), jnp.float32)
    lax.fori_loop(0, shard, step, (zero,) * modes, unroll=2)


def by_step(x, s, steps, rows):
    return jnp.concatenate([x[b * steps + s:b * steps + s + 1] for b in range(rows)], axis=0)


def owner_kernel(width, shard, steps, got, rate_ref, res_ref, skip_ref, back):
    owner = lax.axis_index("seq")
    group, part = owner // 4, owner % 4
    turn = (LANES - 32 * part) % LANES
    quarter = quarter_of((SUB, LANES))

    def four(a, b, c, d):
        b, c, d = pltpu.roll(b, 32, 1), pltpu.roll(c, 64, 1), pltpu.roll(d, 96, 1)
        quarter = quarter_of(a.shape)
        return jnp.where(quarter == 0, a, jnp.where(quarter == 1, b, jnp.where(quarter == 2, c, d)))

    def packed(ref):
        own = ref[:, pl.ds(pl.multiple_of(group * LANES, LANES), LANES)]
        own = pltpu.roll(own, turn, 1)
        low, high = own[:SUB], own[SUB:]
        return four(low, high, low, high)

    rate = packed(rate_ref)
    res = packed(res_ref)
    jump = jnp.exp(-rate * shard)
    carried = jnp.zeros((SUB, LANES), jnp.float32)
    total = jnp.zeros((SUB, LANES), jnp.float32)
    for i in range(got.shape[0]):
        both = got[i].astype(jnp.float32)
        sent = carried.astype(jnp.bfloat16)
        for n in range(4):
            back[i, n] = sent[2 * n:2 * n + 2]
        carried = jump * carried + both[:SUB]
        total = total + both[SUB:]
    scale = lax.rsqrt(pltpu.roll(total, 32, 1) / width + EPS)
    query = rounded(total * scale)
    key = rounded(pltpu.roll(total, 96, 1) * scale)
    value = rounded(pltpu.roll(total, 64, 1) * scale)
    weight = rounded(key * value)
    weight = four(weight, weight, weight, weight)
    skip = jnp.broadcast_to(skip_ref[pl.ds(group, 1), :], (SUB, LANES))
    skip = pltpu.roll(skip, turn, 1)
    skip = four(skip, skip, skip, skip)
    decay = jnp.exp(-rate)
    row = lax.broadcasted_iota(jnp.int32, (SUB, LANES), 0)
    conv = jnp.zeros((SUB, LANES), jnp.float32)
    for s in range(steps):
        first = jnp.broadcast_to(weight[s:s + 1], (SUB, LANES))
        second = jnp.broadcast_to(weight[steps + s:steps + s + 1], (SUB, LANES))
        w = jnp.where(quarter < 2, first, second)
        carried = decay * carried + w
        summed = jnp.broadcast_to(jnp.sum(res * carried, axis=0, keepdims=True), (SUB, LANES))
        summed = summed + pltpu.roll(summed, 96, 1) + skip * w
        conv = jnp.where(row == s, summed, conv)
        conv = jnp.where(row == steps + s, pltpu.roll(summed, 64, 1), conv)
    mix = rounded(query * conv)
    rows = SUB // steps
    mix = four(*[by_step(mix, s, steps, rows) for s in range(steps)]).astype(jnp.bfloat16)
    for i in range(got.shape[0]):
        back[i, 4] = mix


def decode_kernel(mix_ref, w_ref, out):
    pieces = []
    for g in range(mix_ref.shape[0] // 4):
        pieces.append(jnp.concatenate(spread([mix_ref[g * 4 + q, 0].astype(jnp.float32) for q in range(4)]), axis=0))
    mix = jnp.concatenate(pieces, axis=1).astype(jnp.bfloat16)
    out[...] = jnp.dot(mix, w_ref[...], preferred_element_type=jnp.float32)


def add_kernel(a, b, out):
    out[...] = a[...] + b[...]


def finish_kernel(steps, a, b, out):
    total = pltpu.roll(a[...] + b[...], (LANES - 32 * lax.axis_index("chan")) % LANES, 1)
    rows = SUB // steps
    for s in range(steps):
        out[:, s, :] = total[s * rows:(s + 1) * rows, :32].astype(jnp.bfloat16)


def last_kernel(modes, shard, carry_ref, near_ref, q_ref, rate_ref, res_ref, *rest):
    out, trans, decay, weight, state = rest[-5:]
    batch = q_ref.shape[1]
    fill(decay, rate_ref, batch, lambda x: jnp.exp(-x))
    fill(weight, res_ref, batch, lambda x: x)
    for g in range(GROUPS):
        tiles = [jnp.concatenate([carry_ref[g * 4 + q, n].astype(jnp.float32) for n in range(4)], axis=0) for q in range(4)]
        tiles = spread(tiles)
        for r in range(4):
            state[pl.ds((r // 2) * GROUPS + g + (r % 2) * SUB * PAD, SUB, stride=PAD), :] = tiles[r]
    rates, weights = tiles_of(decay, modes), tiles_of(weight, modes)

    def step(t, held):
        trans[pl.ds(t, SUB, stride=PITCH), :] = pairs_sum(list(held) + [near_ref[0, t]])
        return tuple(rates[m] * held[m] for m in range(modes))

    held = tuple(weights[m] * (rates[m] * state[m * PAD:m * PAD + SUB, :]) for m in range(modes))
    lax.fori_loop(0, shard, step, held, unroll=4)
    for b in range(batch):
        for g in range(GROUPS):
            rows = slice(g * LANES, (g + 1) * LANES)
            conv = trans[pl.ds((b * GROUPS + g) * PITCH, shard), :].T
            out[b, rows] = (q_ref[0, b, rows].astype(jnp.float32) * conv).astype(jnp.bfloat16)


def body(features, offsets, tokens, decay_rate, residue, skip_weight, embedding, norm_gain, dec_weight, out_weight):
    _, batch, chans, shard = features.shape
    modes = decay_rate.shape[0]
    steps = tokens.shape[1]
    vocab = embedding.shape[0]
    devices = lax.axis_size("seq")
    width = devices * norm_gain.shape[0]
    block = GROUPS * LANES
    parts = chans // block
    f32 = jnp.float32
    gain = norm_gain.reshape(1, -1)
    skip = skip_weight.reshape(chans // LANES, LANES)
    per_mode = pltpu.VMEM((modes * PAD, LANES), f32)
    across = pltpu.VMEM((SUB * PITCH, LANES), f32)
    by_part = pl.BlockSpec((modes, block), lambda h, *_: (0, h))
    in_time = pl.BlockSpec((1, shard, SUB, LANES), lambda h, *_: (h, 0, 0, 0))
    wide = pltpu.CompilerParams(vmem_limit_bytes=WIDE_LIMIT)
    limit = pltpu.CompilerParams(vmem_limit_bytes=VMEM_LIMIT)

    u_t, send = pl.pallas_call(
        lambda *refs: first_kernel(modes, shard, *refs),
        grid_spec=pltpu.PrefetchScalarGridSpec(
            num_scalar_prefetch=2,
            grid=(parts,),
            in_specs=[
                pl.BlockSpec((1, batch, block, shard), lambda h, *_: (1, 0, h, 0)),
                pl.BlockSpec((1, batch, block, shard), lambda h, *_: (2, 0, h, 0)),
                by_part,
                pl.BlockSpec((vocab, shard), lambda h, *_: (0, 0)),
                pl.BlockSpec((1, shard), lambda h, *_: (0, 0)),
                pl.BlockSpec((3, shard, block), lambda h, *_: (0, 0, h)),
            ],
            out_specs=[in_time, pl.BlockSpec((devices // parts, 2 * SUB, LANES), lambda h, *_: (h, 0, 0))],
            scratch_shapes=[across, per_mode, per_mode, pltpu.VMEM((16, shard), jnp.bfloat16), pltpu.VMEM((SUB, LANES), f32), pltpu.VMEM((GROUPS * 4, SUB, LANES), f32)],
        ),
        out_shape=[
            jax.ShapeDtypeStruct((parts, shard, SUB, LANES), f32),
            jax.ShapeDtypeStruct((devices, 2 * SUB, LANES), jnp.bfloat16),
        ],
        compiler_params=wide,
        name="first",
    )(tokens, offsets, features, features, decay_rate, embedding, gain, dec_weight)

    got = lax.all_to_all(send, "seq", split_axis=0, concat_axis=0, tiled=True)

    halved = parts // 2

    def local(first, rate):
        shifted = pl.BlockSpec((modes, block), lambda h: (0, h + first))
        return pl.pallas_call(
            lambda *refs: local_kernel(modes, shard, *refs),
            grid=(halved,),
            in_specs=[
                pl.BlockSpec((1, shard, SUB, LANES), lambda h: (h + first, 0, 0, 0)),
                shifted,
                shifted,
                pl.BlockSpec((1, GROUPS, LANES), lambda h: (h + first, 0, 0)),
            ],
            out_specs=in_time,
            out_shape=jax.ShapeDtypeStruct((halved, shard, SUB, LANES), f32),
            scratch_shapes=[per_mode, per_mode],
            compiler_params=wide,
            cost_estimate=pl.CostEstimate(flops=2**24, bytes_accessed=2**21, transcendentals=0),
            name="local",
        )(u_t, rate, residue, skip.reshape(parts, GROUPS, LANES))

    near = [local(0, decay_rate)]
    got, near[0] = lax.optimization_barrier((got, near[0]))
    back = pl.pallas_call(
        lambda *refs: owner_kernel(width, shard, steps, *refs),
        out_shape=jax.ShapeDtypeStruct((devices, 5, 2, LANES), jnp.bfloat16),
        compiler_params=limit,
        name="owner",
    )(got, decay_rate, residue, skip)

    back, rate = lax.optimization_barrier((back, decay_rate))
    given = lax.all_to_all(back, "seq", split_axis=0, concat_axis=0, tiled=True)
    near.append(local(halved, rate))
    given, near[1] = lax.optimization_barrier((given, near[1]))

    def trade(x, pairs):
        return lax.ppermute(x, "chan", pairs + [(b, a) for a, b in pairs])

    tile = jax.ShapeDtypeStruct((SUB, LANES), f32)
    partial = pl.pallas_call(
        decode_kernel,
        grid=(1,),
        in_specs=[
            pl.BlockSpec((devices, 1, 2, LANES), lambda i: (0, 4, 0, 0)),
            pl.BlockSpec((chans, LANES), lambda i: (0, 0)),
        ],
        out_specs=pl.BlockSpec((SUB, LANES), lambda i: (0, 0)),
        out_shape=tile,
        compiler_params=limit,
        name="decode",
    )(given, out_weight)
    other = trade(partial, [(0, 1), (2, 3)])

    def last(first, count, rate, *made):
        shifted = pl.BlockSpec((modes, block), lambda h: (0, h + first))
        return pl.pallas_call(
            lambda *refs: last_kernel(modes, shard, *refs),
            grid=(count,),
            in_specs=[
                pl.BlockSpec((devices // parts, 4, 2, LANES), lambda h: (h + first, 0, 0, 0)),
                in_time,
                pl.BlockSpec((1, batch, block, shard), lambda h: (0, 0, h + first, 0)),
                shifted,
                shifted,
            ] + [pl.BlockSpec(memory_space=pl.ANY)] * len(made),
            out_specs=pl.BlockSpec((batch, block, shard), lambda h: (0, h + first, 0)),
            out_shape=jax.ShapeDtypeStruct((batch, chans, shard), jnp.bfloat16),
            scratch_shapes=[across, per_mode, per_mode, per_mode],
            input_output_aliases={5: 0} if made else {},
            compiler_params=wide,
            cost_estimate=pl.CostEstimate(flops=2**24, bytes_accessed=2**21, transcendentals=0),
            name="last",
        )(given, near[first // count], features, rate, residue, *made)

    mixed = last(0, parts // 2, decay_rate)
    other, mixed = lax.optimization_barrier((other, mixed))
    pair = pl.pallas_call(add_kernel, out_shape=tile, compiler_params=limit, name="add")(partial, other)
    pair, rate = lax.optimization_barrier((pair, decay_rate))
    other = trade(pair, [(0, 3), (1, 2)])
    mixed = last(parts // 2, parts // 2, rate, mixed)

    decoded = pl.pallas_call(
        lambda *refs: finish_kernel(steps, *refs),
        out_shape=jax.ShapeDtypeStruct((batch, steps, 32), jnp.bfloat16),
        compiler_params=limit,
        name="finish",
    )(pair, other)
    return (mixed, decoded)


def solution(mesh):
    placed = (
        P(None, None, "chan", "seq"),
        P(),
        P(),
        P(None, "chan"),
        P(None, "chan"),
        P("chan"),
        P(None, "seq"),
        P("seq"),
        P(None, "seq", "chan"),
        P("chan", "seq"),
    )
    return jax.shard_map(
        body,
        mesh=mesh,
        in_specs=placed,
        out_specs=(P(None, "chan", "seq"), P(None, None, ("seq", "chan"))),
        check_vma=False,
    )
```

```python
import jax
import jax.numpy as jnp
from jax import lax
from jax.experimental import pallas as pl
from jax.experimental.pallas import tpu as pltpu
from jax.sharding import PartitionSpec as P

LANES = 128
SUB = 8
GROUPS = 4
PAD = 9
PITCH = 132
EPS = 1e-05
VMEM_LIMIT = 8 * 2**20
WIDE_LIMIT = 60 * 2**20
LAST_LIMIT = 50 * 2**20


def quarter_of(shape):
    return lax.broadcasted_iota(jnp.int32, shape, len(shape) - 1) // 32


def spread(tiles):
    lane = lax.broadcasted_iota(jnp.int32, tiles[0].shape, 1)
    low, even = lane < 64, (lane // 32) % 2 == 0
    made = list(tiles)
    for r in range(2):
        a, b = tiles[r], tiles[r + 2]
        made[r] = jnp.where(low, a, pltpu.roll(b, 64, 1))
        made[r + 2] = jnp.where(low, pltpu.roll(a, 64, 1), b)
    for r in (0, 2):
        a, b = made[r], made[r + 1]
        made[r] = jnp.where(even, a, pltpu.roll(b, 32, 1))
        made[r + 1] = jnp.where(even, pltpu.roll(a, 96, 1), b)
    return made


def rounded(x):
    return x.astype(jnp.bfloat16).astype(jnp.float32)


def pairs_sum(terms):
    while len(terms) > 1:
        terms = [x + y for x, y in zip(terms[::2], terms[1::2])] + terms[len(terms) // 2 * 2:]
    return terms[0]


def fill(scratch, ref, batch, fn):
    modes = ref.shape[0]
    for g in range(GROUPS):
        values = fn(ref[:, g * LANES:(g + 1) * LANES])
        for b in range(batch):
            scratch[pl.ds(b * GROUPS + g, modes, stride=PAD), :] = values


def tiles_of(scratch, modes):
    return [scratch[m * PAD:m * PAD + SUB, :] for m in range(modes)]


def first_kernel(modes, shard, tokens, offsets, k_ref, v_ref, rate_ref, emb_ref, gain_ref, w_ref,
                 u_out, send, trans, decay, state, x16, squares, sums):
    part = pl.program_id(0)
    position = lax.axis_index("seq") * shard + lax.broadcasted_iota(jnp.int32, (LANES, shard), 1)
    batch = k_ref.shape[1]
    steps = tokens.shape[1]
    count = batch * steps

    @pl.when(part == 0)
    def _():
        vocab = emb_ref.shape[0]
        row = lax.broadcasted_iota(jnp.int32, (16, vocab), 0)
        wanted = jnp.full((16, vocab), -1, jnp.int32)
        for t in range(count):
            wanted = jnp.where(row == t, tokens[t // steps, t % steps], wanted)
        hot = (lax.broadcasted_iota(jnp.int32, (16, vocab), 1) == wanted).astype(jnp.float32)
        x = jnp.dot(hot.astype(jnp.bfloat16), emb_ref[...], preferred_element_type=jnp.float32)[:SUB]
        squares[...] = jnp.broadcast_to(jnp.sum(x * x, axis=1, keepdims=True), (SUB, LANES))
        scaled = x * gain_ref[...]
        high = rounded(scaled)
        x16[...] = jnp.concatenate([high, scaled - high], axis=0).astype(jnp.bfloat16)

    fill(decay, rate_ref, batch, lambda x: jnp.exp(-x))
    for b in range(batch):
        live = (position >= offsets[b]).astype(jnp.float32).astype(jnp.bfloat16) > 0
        for g in range(GROUPS):
            rows = slice(g * LANES, (g + 1) * LANES)
            u = jnp.where(live, k_ref[0, b, rows] * v_ref[0, b, rows], jnp.bfloat16(0))
            trans[pl.ds((b * GROUPS + g) * PITCH, shard), :] = u.astype(jnp.float32).T

    terms = []
    for i in range(3):
        both = jnp.dot(x16[...], w_ref[i], preferred_element_type=jnp.float32)
        terms.append(both[:SUB] + both[SUB:])
    for g in range(GROUPS):
        parts = spread([t[:, g * LANES:(g + 1) * LANES] for t in terms] + [squares[...]])
        for q in range(4):
            sums[g * 4 + q] = parts[q]

    rates = tiles_of(decay, modes)

    def step(t, held):
        u = trans[pl.ds(t, SUB, stride=PITCH), :]
        u_out[0, t] = u
        return tuple(rates[m] * held[m] + u for m in range(modes))

    zero = jnp.zeros((SUB, LANES), jnp.float32)
    held = lax.fori_loop(0, shard, step, (zero,) * modes, unroll=4)
    for m in range(modes):
        state[m * PAD:m * PAD + SUB, :] = held[m]

    for g in range(GROUPS):
        ends = [state[pl.ds((r // 2) * GROUPS + g + (r % 2) * SUB * PAD, SUB, stride=PAD), :] for r in range(4)]
        for q, tile in enumerate(spread(ends)):
            send[g * 4 + q] = jnp.concatenate([tile, sums[g * 4 + q]], axis=0).astype(jnp.bfloat16)


def local_kernel(modes, shard, u_ref, rate_ref, res_ref, skip_ref, q_ref, out, rate_out, gain_out, q_out, decay, weight):
    batch = SUB // GROUPS
    fill(decay, rate_ref, batch, lambda x: jnp.exp(-x))
    fill(weight, res_ref, batch, lambda x: x)
    rates, weights = tiles_of(decay, modes), tiles_of(weight, modes)
    q_out[...] = q_ref[...]
    for m in range(modes):
        rate_out[0, m] = rates[m]
        gain_out[0, m] = rates[m] * weights[m]
    skip = jnp.concatenate([skip_ref[0]] * batch, axis=0)

    def step(t, held):
        u = u_ref[0, t]
        held = tuple(rates[m] * held[m] + u for m in range(modes))
        out[0, t] = pairs_sum([weights[m] * held[m] for m in range(modes)] + [skip * u])
        return held

    zero = jnp.zeros((SUB, LANES), jnp.float32)
    lax.fori_loop(0, shard, step, (zero,) * modes, unroll=2)


def by_step(x, s, steps, rows):
    return jnp.concatenate([x[b * steps + s:b * steps + s + 1] for b in range(rows)], axis=0)


def owner_kernel(width, shard, steps, got, rate_ref, res_ref, skip_ref, back):
    owner = lax.axis_index("seq")
    group, part = owner // 4, owner % 4
    turn = (LANES - 32 * part) % LANES
    quarter = quarter_of((SUB, LANES))

    def four(a, b, c, d):
        b, c, d = pltpu.roll(b, 32, 1), pltpu.roll(c, 64, 1), pltpu.roll(d, 96, 1)
        quarter = quarter_of(a.shape)
        return jnp.where(quarter == 0, a, jnp.where(quarter == 1, b, jnp.where(quarter == 2, c, d)))

    def packed(ref):
        own = ref[:, pl.ds(pl.multiple_of(group * LANES, LANES), LANES)]
        own = pltpu.roll(own, turn, 1)
        low, high = own[:SUB], own[SUB:]
        return four(low, high, low, high)

    rate = packed(rate_ref)
    res = packed(res_ref)
    jump = jnp.exp(-rate * shard)
    carried = jnp.zeros((SUB, LANES), jnp.float32)
    total = jnp.zeros((SUB, LANES), jnp.float32)
    for i in range(got.shape[0]):
        both = got[i].astype(jnp.float32)
        sent = carried.astype(jnp.bfloat16)
        for n in range(4):
            back[i, n] = sent[2 * n:2 * n + 2]
        carried = jump * carried + both[:SUB]
        total = total + both[SUB:]
    scale = lax.rsqrt(pltpu.roll(total, 32, 1) / width + EPS)
    query = rounded(total * scale)
    key = rounded(pltpu.roll(total, 96, 1) * scale)
    value = rounded(pltpu.roll(total, 64, 1) * scale)
    weight = rounded(key * value)
    weight = four(weight, weight, weight, weight)
    skip = jnp.broadcast_to(skip_ref[pl.ds(group, 1), :], (SUB, LANES))
    skip = pltpu.roll(skip, turn, 1)
    skip = four(skip, skip, skip, skip)
    decay = jnp.exp(-rate)
    row = lax.broadcasted_iota(jnp.int32, (SUB, LANES), 0)
    conv = jnp.zeros((SUB, LANES), jnp.float32)
    for s in range(steps):
        first = jnp.broadcast_to(weight[s:s + 1], (SUB, LANES))
        second = jnp.broadcast_to(weight[steps + s:steps + s + 1], (SUB, LANES))
        w = jnp.where(quarter < 2, first, second)
        carried = decay * carried + w
        summed = jnp.broadcast_to(jnp.sum(res * carried, axis=0, keepdims=True), (SUB, LANES))
        summed = summed + pltpu.roll(summed, 96, 1) + skip * w
        conv = jnp.where(row == s, summed, conv)
        conv = jnp.where(row == steps + s, pltpu.roll(summed, 64, 1), conv)
    mix = rounded(query * conv)
    rows = SUB // steps
    mix = four(*[by_step(mix, s, steps, rows) for s in range(steps)]).astype(jnp.bfloat16)
    for i in range(got.shape[0]):
        back[i, 4] = mix


def decode_kernel(mix_ref, w_ref, out):
    pieces = []
    for g in range(mix_ref.shape[0] // 4):
        pieces.append(jnp.concatenate(spread([mix_ref[g * 4 + q, 0].astype(jnp.float32) for q in range(4)]), axis=0))
    mix = jnp.concatenate(pieces, axis=1).astype(jnp.bfloat16)
    out[...] = jnp.dot(mix, w_ref[...], preferred_element_type=jnp.float32)


def add_kernel(a, b, out):
    out[...] = a[...] + b[...]


def finish_kernel(steps, a, b, out):
    total = pltpu.roll(a[...] + b[...], (LANES - 32 * lax.axis_index("chan")) % LANES, 1)
    rows = SUB // steps
    for s in range(steps):
        out[:, s, :] = total[s * rows:(s + 1) * rows, :32].astype(jnp.bfloat16)


def last_kernel(modes, shard, carry_ref, near_ref, rate_ref, gain_ref, q_ref, *rest):
    out, trans, state = rest[-3:]
    batch = q_ref.shape[1]
    for g in range(GROUPS):
        tiles = [carry_ref[g * 4 + q].astype(jnp.float32).reshape(SUB, LANES) for q in range(4)]
        tiles = spread(tiles)
        for r in range(4):
            state[pl.ds((r // 2) * GROUPS + g + (r % 2) * SUB * PAD, SUB, stride=PAD), :] = tiles[r]
    rates = [rate_ref[0, m] for m in range(modes)]

    def step(t, held):
        trans[pl.ds(t, SUB, stride=PITCH), :] = pairs_sum(list(held) + [near_ref[0, t]])
        return tuple(rates[m] * held[m] for m in range(modes))

    held = tuple(gain_ref[0, m] * state[m * PAD:m * PAD + SUB, :] for m in range(modes))
    lax.fori_loop(0, shard, step, held, unroll=4)
    for b in range(batch):
        for g in range(GROUPS):
            rows = slice(g * LANES, (g + 1) * LANES)
            conv = trans[pl.ds((b * GROUPS + g) * PITCH, shard), :].T
            out[b, rows] = (q_ref[0, b, rows].astype(jnp.float32) * conv).astype(jnp.bfloat16)


def body(features, offsets, tokens, decay_rate, residue, skip_weight, embedding, norm_gain, dec_weight, out_weight):
    _, batch, chans, shard = features.shape
    modes = decay_rate.shape[0]
    steps = tokens.shape[1]
    vocab = embedding.shape[0]
    devices = lax.axis_size("seq")
    width = devices * norm_gain.shape[0]
    block = GROUPS * LANES
    parts = chans // block
    f32 = jnp.float32
    gain = norm_gain.reshape(1, -1)
    skip = skip_weight.reshape(chans // LANES, LANES)
    per_mode = pltpu.VMEM((modes * PAD, LANES), f32)
    across = pltpu.VMEM((SUB * PITCH, LANES), f32)
    by_part = pl.BlockSpec((modes, block), lambda h, *_: (0, h))
    in_time = pl.BlockSpec((1, shard, SUB, LANES), lambda h, *_: (h, 0, 0, 0))
    wide = pltpu.CompilerParams(vmem_limit_bytes=WIDE_LIMIT)
    limit = pltpu.CompilerParams(vmem_limit_bytes=VMEM_LIMIT)

    u_t, send = pl.pallas_call(
        lambda *refs: first_kernel(modes, shard, *refs),
        grid_spec=pltpu.PrefetchScalarGridSpec(
            num_scalar_prefetch=2,
            grid=(parts,),
            in_specs=[
                pl.BlockSpec((1, batch, block, shard), lambda h, *_: (1, 0, h, 0)),
                pl.BlockSpec((1, batch, block, shard), lambda h, *_: (2, 0, h, 0)),
                by_part,
                pl.BlockSpec((vocab, shard), lambda h, *_: (0, 0)),
                pl.BlockSpec((1, shard), lambda h, *_: (0, 0)),
                pl.BlockSpec((3, shard, block), lambda h, *_: (0, 0, h)),
            ],
            out_specs=[in_time, pl.BlockSpec((devices // parts, 2 * SUB, LANES), lambda h, *_: (h, 0, 0))],
            scratch_shapes=[across, per_mode, per_mode, pltpu.VMEM((16, shard), jnp.bfloat16), pltpu.VMEM((SUB, LANES), f32), pltpu.VMEM((GROUPS * 4, SUB, LANES), f32)],
        ),
        out_shape=[
            jax.ShapeDtypeStruct((parts, shard, SUB, LANES), f32),
            jax.ShapeDtypeStruct((devices, 2 * SUB, LANES), jnp.bfloat16),
        ],
        compiler_params=wide,
        name="first",
    )(tokens, offsets, features, features, decay_rate, embedding, gain, dec_weight)

    got = lax.all_to_all(send, "seq", split_axis=0, concat_axis=0, tiled=True)

    halved = parts // 2
    own = pl.BlockSpec((1, batch, block, shard), lambda h: (h, 0, 0, 0))
    tiles = pl.BlockSpec((1, modes, SUB, LANES), lambda h: (h, 0, 0, 0))

    def local(first, rate):
        shifted = pl.BlockSpec((modes, block), lambda h: (0, h + first))
        return pl.pallas_call(
            lambda *refs: local_kernel(modes, shard, *refs),
            grid=(halved,),
            in_specs=[
                pl.BlockSpec((1, shard, SUB, LANES), lambda h: (h + first, 0, 0, 0)),
                shifted,
                shifted,
                pl.BlockSpec((1, GROUPS, LANES), lambda h: (h + first, 0, 0)),
                pl.BlockSpec((1, batch, block, shard), lambda h: (0, 0, h + first, 0)),
            ],
            out_specs=[in_time, tiles, tiles, own],
            out_shape=[
                jax.ShapeDtypeStruct((halved, shard, SUB, LANES), f32),
                jax.ShapeDtypeStruct((halved, modes, SUB, LANES), f32),
                jax.ShapeDtypeStruct((halved, modes, SUB, LANES), f32),
                jax.ShapeDtypeStruct((halved, batch, block, shard), jnp.bfloat16),
            ],
            scratch_shapes=[per_mode, per_mode],
            compiler_params=wide,
            cost_estimate=pl.CostEstimate(flops=2**24, bytes_accessed=2**21, transcendentals=0),
            name="local",
        )(u_t, rate, residue, skip.reshape(parts, GROUPS, LANES), features)

    near = [local(0, decay_rate)]
    got, near[0] = lax.optimization_barrier((got, tuple(near[0])))
    back = pl.pallas_call(
        lambda *refs: owner_kernel(width, shard, steps, *refs),
        out_shape=jax.ShapeDtypeStruct((devices, 5, 2, LANES), jnp.bfloat16),
        compiler_params=limit,
        name="owner",
    )(got, decay_rate, residue, skip)

    back, rate = lax.optimization_barrier((back, decay_rate))
    given = lax.all_to_all(back, "seq", split_axis=0, concat_axis=0, tiled=True)
    near.append(local(halved, rate))
    given, near[1] = lax.optimization_barrier((given, tuple(near[1])))

    def trade(x, pairs):
        return lax.ppermute(x, "chan", pairs + [(b, a) for a, b in pairs])

    tile = jax.ShapeDtypeStruct((SUB, LANES), f32)
    partial = pl.pallas_call(
        decode_kernel,
        grid=(1,),
        in_specs=[
            pl.BlockSpec((devices, 1, 2, LANES), lambda i: (0, 4, 0, 0)),
            pl.BlockSpec((chans, LANES), lambda i: (0, 0)),
        ],
        out_specs=pl.BlockSpec((SUB, LANES), lambda i: (0, 0)),
        out_shape=tile,
        compiler_params=limit,
        name="decode",
    )(given, out_weight)
    other = trade(partial, [(0, 1), (2, 3)])

    def last(first, mine, *made):
        return pl.pallas_call(
            lambda *refs: last_kernel(modes, shard, *refs),
            grid=(halved,),
            in_specs=[
                pl.BlockSpec((devices // parts, 4, 2, LANES), lambda h: (h + first, 0, 0, 0)),
                in_time,
                tiles,
                tiles,
                own,
            ] + [pl.BlockSpec(memory_space=pl.ANY)] * len(made),
            out_specs=pl.BlockSpec((batch, block, shard), lambda h: (0, h + first, 0)),
            out_shape=jax.ShapeDtypeStruct((batch, chans, shard), jnp.bfloat16),
            scratch_shapes=[across, per_mode],
            input_output_aliases={5: 0} if made else {},
            compiler_params=pltpu.CompilerParams(vmem_limit_bytes=LAST_LIMIT),
            cost_estimate=pl.CostEstimate(flops=2**24, bytes_accessed=2**21, transcendentals=0),
            name="last",
        )(given, *mine, *made)

    mixed = last(0, near[0])
    other, mixed = lax.optimization_barrier((other, mixed))
    pair = pl.pallas_call(add_kernel, out_shape=tile, compiler_params=limit, name="add")(partial, other)
    pair, second = lax.optimization_barrier((pair, tuple(near[1])))
    other = trade(pair, [(0, 3), (1, 2)])
    mixed = last(halved, second, mixed)

    decoded = pl.pallas_call(
        lambda *refs: finish_kernel(steps, *refs),
        out_shape=jax.ShapeDtypeStruct((batch, steps, 32), jnp.bfloat16),
        compiler_params=limit,
        name="finish",
    )(pair, other)
    return (mixed, decoded)


def solution(mesh):
    placed = (
        P(None, None, "chan", "seq"),
        P(),
        P(),
        P(None, "chan"),
        P(None, "chan"),
        P("chan"),
        P(None, "seq"),
        P("seq"),
        P(None, "seq", "chan"),
        P("chan", "seq"),
    )
    return jax.shard_map(
        body,
        mesh=mesh,
        in_specs=placed,
        out_specs=(P(None, "chan", "seq"), P(None, None, ("seq", "chan"))),
        check_vma=False,
    )
```

```python
import jax
import jax.numpy as jnp
from jax import lax
from jax.experimental import pallas as pl
from jax.experimental.pallas import tpu as pltpu
from jax.sharding import PartitionSpec as P

LANES = 128
SUB = 8
GROUPS = 4
PAD = 9
PITCH = 132
EPS = 1e-05
VMEM_LIMIT = 8 * 2**20
WIDE_LIMIT = 60 * 2**20
LAST_LIMIT = 50 * 2**20


def quarter_of(shape):
    return lax.broadcasted_iota(jnp.int32, shape, len(shape) - 1) // 32


def spread(tiles):
    lane = lax.broadcasted_iota(jnp.int32, tiles[0].shape, 1)
    low, even = lane < 64, (lane // 32) % 2 == 0
    made = list(tiles)
    for r in range(2):
        a, b = tiles[r], tiles[r + 2]
        made[r] = jnp.where(low, a, pltpu.roll(b, 64, 1))
        made[r + 2] = jnp.where(low, pltpu.roll(a, 64, 1), b)
    for r in (0, 2):
        a, b = made[r], made[r + 1]
        made[r] = jnp.where(even, a, pltpu.roll(b, 32, 1))
        made[r + 1] = jnp.where(even, pltpu.roll(a, 96, 1), b)
    return made


def rounded(x):
    return x.astype(jnp.bfloat16).astype(jnp.float32)


def pairs_sum(terms):
    while len(terms) > 1:
        terms = [x + y for x, y in zip(terms[::2], terms[1::2])] + terms[len(terms) // 2 * 2:]
    return terms[0]


def fill(scratch, ref, batch, fn):
    modes = ref.shape[0]
    for g in range(GROUPS):
        values = fn(ref[:, g * LANES:(g + 1) * LANES])
        for b in range(batch):
            scratch[pl.ds(b * GROUPS + g, modes, stride=PAD), :] = values


def tiles_of(scratch, modes):
    return [scratch[m * PAD:m * PAD + SUB, :] for m in range(modes)]


def first_kernel(modes, shard, tokens, offsets, k_ref, v_ref, rate_ref, emb_ref, gain_ref, w_ref,
                 u_out, send, trans, decay, state, x16, squares, sums):
    part = pl.program_id(0)
    position = lax.axis_index("seq") * shard + lax.broadcasted_iota(jnp.int32, (LANES, shard), 1)
    batch = k_ref.shape[1]
    steps = tokens.shape[1]
    count = batch * steps

    @pl.when(part == 0)
    def _():
        vocab = emb_ref.shape[0]
        row = lax.broadcasted_iota(jnp.int32, (16, vocab), 0)
        wanted = jnp.full((16, vocab), -1, jnp.int32)
        for t in range(count):
            wanted = jnp.where(row == t, tokens[t // steps, t % steps], wanted)
        hot = (lax.broadcasted_iota(jnp.int32, (16, vocab), 1) == wanted).astype(jnp.float32)
        x = jnp.dot(hot.astype(jnp.bfloat16), emb_ref[...], preferred_element_type=jnp.float32)[:SUB]
        squares[...] = jnp.broadcast_to(jnp.sum(x * x, axis=1, keepdims=True), (SUB, LANES))
        scaled = x * gain_ref[...]
        high = rounded(scaled)
        x16[...] = jnp.concatenate([high, scaled - high], axis=0).astype(jnp.bfloat16)

    fill(decay, rate_ref, batch, lambda x: jnp.exp(-x))
    for b in range(batch):
        live = (position >= offsets[b]).astype(jnp.float32).astype(jnp.bfloat16) > 0
        for g in range(GROUPS):
            rows = slice(g * LANES, (g + 1) * LANES)
            u = jnp.where(live, k_ref[0, b, rows] * v_ref[0, b, rows], jnp.bfloat16(0))
            trans[pl.ds((b * GROUPS + g) * PITCH, shard), :] = u.astype(jnp.float32).T

    terms = []
    for i in range(3):
        both = jnp.dot(x16[...], w_ref[i], preferred_element_type=jnp.float32)
        terms.append(both[:SUB] + both[SUB:])
    for g in range(GROUPS):
        parts = spread([t[:, g * LANES:(g + 1) * LANES] for t in terms] + [squares[...]])
        for q in range(4):
            sums[g * 4 + q] = parts[q]

    rates = tiles_of(decay, modes)

    def step(t, held):
        u = trans[pl.ds(t, SUB, stride=PITCH), :]
        u_out[0, t] = u
        return tuple(rates[m] * held[m] + u for m in range(modes))

    zero = jnp.zeros((SUB, LANES), jnp.float32)
    held = lax.fori_loop(0, shard, step, (zero,) * modes, unroll=4)
    for m in range(modes):
        state[m * PAD:m * PAD + SUB, :] = held[m]

    for g in range(GROUPS):
        ends = [state[pl.ds((r // 2) * GROUPS + g + (r % 2) * SUB * PAD, SUB, stride=PAD), :] for r in range(4)]
        for q, tile in enumerate(spread(ends)):
            send[g * 4 + q] = jnp.concatenate([tile, sums[g * 4 + q]], axis=0).astype(jnp.bfloat16)


def local_kernel(modes, shard, u_ref, rate_ref, res_ref, skip_ref, q_ref, out, rate_out, q_out, decay, weight):
    batch = SUB // GROUPS
    fill(decay, rate_ref, batch, lambda x: jnp.exp(-x))
    fill(weight, res_ref, batch, lambda x: x)
    rates, weights = tiles_of(decay, modes), tiles_of(weight, modes)
    q_out[...] = q_ref[...]
    for m in range(modes):
        rate_out[0, m] = rates[m]
    skip = jnp.concatenate([skip_ref[0]] * batch, axis=0)

    def step(t, held):
        u = u_ref[0, t]
        held = tuple(rates[m] * held[m] + u for m in range(modes))
        out[0, t] = pairs_sum([weights[m] * held[m] for m in range(modes)] + [skip * u])
        return held

    zero = jnp.zeros((SUB, LANES), jnp.float32)
    lax.fori_loop(0, shard, step, (zero,) * modes, unroll=2)


def by_step(x, s, steps, rows):
    return jnp.concatenate([x[b * steps + s:b * steps + s + 1] for b in range(rows)], axis=0)


def owner_kernel(width, shard, steps, got, rate_ref, res_ref, skip_ref, back):
    owner = lax.axis_index("seq")
    group, part = owner // 4, owner % 4
    turn = (LANES - 32 * part) % LANES
    quarter = quarter_of((SUB, LANES))

    def four(a, b, c, d):
        b, c, d = pltpu.roll(b, 32, 1), pltpu.roll(c, 64, 1), pltpu.roll(d, 96, 1)
        quarter = quarter_of(a.shape)
        return jnp.where(quarter == 0, a, jnp.where(quarter == 1, b, jnp.where(quarter == 2, c, d)))

    def packed(ref):
        own = ref[:, pl.ds(pl.multiple_of(group * LANES, LANES), LANES)]
        own = pltpu.roll(own, turn, 1)
        low, high = own[:SUB], own[SUB:]
        return four(low, high, low, high)

    rate = packed(rate_ref)
    res = packed(res_ref)
    jump = jnp.exp(-rate * shard)
    gain = res * jnp.exp(-rate)
    carried = jnp.zeros((SUB, LANES), jnp.float32)
    total = jnp.zeros((SUB, LANES), jnp.float32)
    for i in range(got.shape[0]):
        both = got[i].astype(jnp.float32)
        sent = (gain * carried).astype(jnp.bfloat16)
        for n in range(4):
            back[i, n] = sent[2 * n:2 * n + 2]
        carried = jump * carried + both[:SUB]
        total = total + both[SUB:]
    scale = lax.rsqrt(pltpu.roll(total, 32, 1) / width + EPS)
    query = rounded(total * scale)
    key = rounded(pltpu.roll(total, 96, 1) * scale)
    value = rounded(pltpu.roll(total, 64, 1) * scale)
    weight = rounded(key * value)
    weight = four(weight, weight, weight, weight)
    skip = jnp.broadcast_to(skip_ref[pl.ds(group, 1), :], (SUB, LANES))
    skip = pltpu.roll(skip, turn, 1)
    skip = four(skip, skip, skip, skip)
    decay = jnp.exp(-rate)
    row = lax.broadcasted_iota(jnp.int32, (SUB, LANES), 0)
    conv = jnp.zeros((SUB, LANES), jnp.float32)
    for s in range(steps):
        first = jnp.broadcast_to(weight[s:s + 1], (SUB, LANES))
        second = jnp.broadcast_to(weight[steps + s:steps + s + 1], (SUB, LANES))
        w = jnp.where(quarter < 2, first, second)
        carried = decay * carried + w
        summed = jnp.broadcast_to(jnp.sum(res * carried, axis=0, keepdims=True), (SUB, LANES))
        summed = summed + pltpu.roll(summed, 96, 1) + skip * w
        conv = jnp.where(row == s, summed, conv)
        conv = jnp.where(row == steps + s, pltpu.roll(summed, 64, 1), conv)
    mix = rounded(query * conv)
    rows = SUB // steps
    mix = four(*[by_step(mix, s, steps, rows) for s in range(steps)]).astype(jnp.bfloat16)
    for i in range(got.shape[0]):
        back[i, 4] = mix


def decode_kernel(mix_ref, w_ref, out):
    pieces = []
    for g in range(mix_ref.shape[0] // 4):
        pieces.append(jnp.concatenate(spread([mix_ref[g * 4 + q, 0].astype(jnp.float32) for q in range(4)]), axis=0))
    mix = jnp.concatenate(pieces, axis=1).astype(jnp.bfloat16)
    out[...] = jnp.dot(mix, w_ref[...], preferred_element_type=jnp.float32)


def add_kernel(a, b, out):
    out[...] = a[...] + b[...]


def finish_kernel(steps, a, b, out):
    total = pltpu.roll(a[...] + b[...], (LANES - 32 * lax.axis_index("chan")) % LANES, 1)
    rows = SUB // steps
    for s in range(steps):
        out[:, s, :] = total[s * rows:(s + 1) * rows, :32].astype(jnp.bfloat16)


def last_kernel(modes, shard, carry_ref, near_ref, rate_ref, q_ref, *rest):
    out, trans, state = rest[-3:]
    batch = q_ref.shape[1]
    for g in range(GROUPS):
        tiles = [carry_ref[g * 4 + q].astype(jnp.float32).reshape(SUB, LANES) for q in range(4)]
        tiles = spread(tiles)
        for r in range(4):
            state[pl.ds((r // 2) * GROUPS + g + (r % 2) * SUB * PAD, SUB, stride=PAD), :] = tiles[r]
    rates = [rate_ref[0, m] for m in range(modes)]

    def step(t, held):
        trans[pl.ds(t, SUB, stride=PITCH), :] = pairs_sum(list(held) + [near_ref[0, t]])
        return tuple(rates[m] * held[m] for m in range(modes))

    held = tuple(state[m * PAD:m * PAD + SUB, :] for m in range(modes))
    lax.fori_loop(0, shard, step, held, unroll=4)
    for b in range(batch):
        for g in range(GROUPS):
            rows = slice(g * LANES, (g + 1) * LANES)
            conv = trans[pl.ds((b * GROUPS + g) * PITCH, shard), :].T
            out[b, rows] = (q_ref[0, b, rows].astype(jnp.float32) * conv).astype(jnp.bfloat16)


def body(features, offsets, tokens, decay_rate, residue, skip_weight, embedding, norm_gain, dec_weight, out_weight):
    _, batch, chans, shard = features.shape
    modes = decay_rate.shape[0]
    steps = tokens.shape[1]
    vocab = embedding.shape[0]
    devices = lax.axis_size("seq")
    width = devices * norm_gain.shape[0]
    block = GROUPS * LANES
    parts = chans // block
    f32 = jnp.float32
    gain = norm_gain.reshape(1, -1)
    skip = skip_weight.reshape(chans // LANES, LANES)
    per_mode = pltpu.VMEM((modes * PAD, LANES), f32)
    across = pltpu.VMEM((SUB * PITCH, LANES), f32)
    by_part = pl.BlockSpec((modes, block), lambda h, *_: (0, h))
    in_time = pl.BlockSpec((1, shard, SUB, LANES), lambda h, *_: (h, 0, 0, 0))
    wide = pltpu.CompilerParams(vmem_limit_bytes=WIDE_LIMIT)
    limit = pltpu.CompilerParams(vmem_limit_bytes=VMEM_LIMIT)

    u_t, send = pl.pallas_call(
        lambda *refs: first_kernel(modes, shard, *refs),
        grid_spec=pltpu.PrefetchScalarGridSpec(
            num_scalar_prefetch=2,
            grid=(parts,),
            in_specs=[
                pl.BlockSpec((1, batch, block, shard), lambda h, *_: (1, 0, h, 0)),
                pl.BlockSpec((1, batch, block, shard), lambda h, *_: (2, 0, h, 0)),
                by_part,
                pl.BlockSpec((vocab, shard), lambda h, *_: (0, 0)),
                pl.BlockSpec((1, shard), lambda h, *_: (0, 0)),
                pl.BlockSpec((3, shard, block), lambda h, *_: (0, 0, h)),
            ],
            out_specs=[in_time, pl.BlockSpec((devices // parts, 2 * SUB, LANES), lambda h, *_: (h, 0, 0))],
            scratch_shapes=[across, per_mode, per_mode, pltpu.VMEM((16, shard), jnp.bfloat16), pltpu.VMEM((SUB, LANES), f32), pltpu.VMEM((GROUPS * 4, SUB, LANES), f32)],
        ),
        out_shape=[
            jax.ShapeDtypeStruct((parts, shard, SUB, LANES), f32),
            jax.ShapeDtypeStruct((devices, 2 * SUB, LANES), jnp.bfloat16),
        ],
        compiler_params=wide,
        name="first",
    )(tokens, offsets, features, features, decay_rate, embedding, gain, dec_weight)

    got = lax.all_to_all(send, "seq", split_axis=0, concat_axis=0, tiled=True)

    halved = parts // 2
    own = pl.BlockSpec((1, batch, block, shard), lambda h: (h, 0, 0, 0))
    tiles = pl.BlockSpec((1, modes, SUB, LANES), lambda h: (h, 0, 0, 0))

    def local(first, rate):
        shifted = pl.BlockSpec((modes, block), lambda h: (0, h + first))
        return pl.pallas_call(
            lambda *refs: local_kernel(modes, shard, *refs),
            grid=(halved,),
            in_specs=[
                pl.BlockSpec((1, shard, SUB, LANES), lambda h: (h + first, 0, 0, 0)),
                shifted,
                shifted,
                pl.BlockSpec((1, GROUPS, LANES), lambda h: (h + first, 0, 0)),
                pl.BlockSpec((1, batch, block, shard), lambda h: (0, 0, h + first, 0)),
            ],
            out_specs=[in_time, tiles, own],
            out_shape=[
                jax.ShapeDtypeStruct((halved, shard, SUB, LANES), f32),
                jax.ShapeDtypeStruct((halved, modes, SUB, LANES), f32),
                jax.ShapeDtypeStruct((halved, batch, block, shard), jnp.bfloat16),
            ],
            scratch_shapes=[per_mode, per_mode],
            compiler_params=wide,
            cost_estimate=pl.CostEstimate(flops=2**24, bytes_accessed=2**21, transcendentals=0),
            name="local",
        )(u_t, rate, residue, skip.reshape(parts, GROUPS, LANES), features)

    near = [local(0, decay_rate)]
    got, near[0] = lax.optimization_barrier((got, tuple(near[0])))
    back = pl.pallas_call(
        lambda *refs: owner_kernel(width, shard, steps, *refs),
        out_shape=jax.ShapeDtypeStruct((devices, 5, 2, LANES), jnp.bfloat16),
        compiler_params=limit,
        name="owner",
    )(got, decay_rate, residue, skip)

    back, rate = lax.optimization_barrier((back, decay_rate))
    given = lax.all_to_all(back, "seq", split_axis=0, concat_axis=0, tiled=True)
    near.append(local(halved, rate))
    given, near[1] = lax.optimization_barrier((given, tuple(near[1])))

    def trade(x, pairs):
        return lax.ppermute(x, "chan", pairs + [(b, a) for a, b in pairs])

    tile = jax.ShapeDtypeStruct((SUB, LANES), f32)
    partial = pl.pallas_call(
        decode_kernel,
        grid=(1,),
        in_specs=[
            pl.BlockSpec((devices, 1, 2, LANES), lambda i: (0, 4, 0, 0)),
            pl.BlockSpec((chans, LANES), lambda i: (0, 0)),
        ],
        out_specs=pl.BlockSpec((SUB, LANES), lambda i: (0, 0)),
        out_shape=tile,
        compiler_params=limit,
        name="decode",
    )(given, out_weight)
    other = trade(partial, [(0, 1), (2, 3)])

    def last(first, mine, *made):
        return pl.pallas_call(
            lambda *refs: last_kernel(modes, shard, *refs),
            grid=(halved,),
            in_specs=[
                pl.BlockSpec((devices // parts, 4, 2, LANES), lambda h: (h + first, 0, 0, 0)),
                in_time,
                tiles,
                own,
            ] + [pl.BlockSpec(memory_space=pl.ANY)] * len(made),
            out_specs=pl.BlockSpec((batch, block, shard), lambda h: (0, h + first, 0)),
            out_shape=jax.ShapeDtypeStruct((batch, chans, shard), jnp.bfloat16),
            scratch_shapes=[across, per_mode],
            input_output_aliases={4: 0} if made else {},
            compiler_params=pltpu.CompilerParams(vmem_limit_bytes=LAST_LIMIT),
            cost_estimate=pl.CostEstimate(flops=2**24, bytes_accessed=2**21, transcendentals=0),
            name="last",
        )(given, *mine, *made)

    mixed = last(0, near[0])
    other, mixed = lax.optimization_barrier((other, mixed))
    pair = pl.pallas_call(add_kernel, out_shape=tile, compiler_params=limit, name="add")(partial, other)
    pair, second = lax.optimization_barrier((pair, tuple(near[1])))
    other = trade(pair, [(0, 3), (1, 2)])
    mixed = last(halved, second, mixed)

    decoded = pl.pallas_call(
        lambda *refs: finish_kernel(steps, *refs),
        out_shape=jax.ShapeDtypeStruct((batch, steps, 32), jnp.bfloat16),
        compiler_params=limit,
        name="finish",
    )(pair, other)
    return (mixed, decoded)


def solution(mesh):
    placed = (
        P(None, None, "chan", "seq"),
        P(),
        P(),
        P(None, "chan"),
        P(None, "chan"),
        P("chan"),
        P(None, "seq"),
        P("seq"),
        P(None, "seq", "chan"),
        P("chan", "seq"),
    )
    return jax.shard_map(
        body,
        mesh=mesh,
        in_specs=placed,
        out_specs=(P(None, "chan", "seq"), P(None, None, ("seq", "chan"))),
        check_vma=False,
    )
```
